1024 devices in a mesh: dp: 4 (over x), ctx: 32 (over z), tp: 8 (over y, core).
Axes of the slice: x: 4, y: 4, z: 32, core: 2. Of those that a mesh axis runs over, the one named last changes fastest.
Arguments:
- queries: bfloat16 [16384, 4096], P(('dp', 'ctx'), 'tp'), parts along dimension 0, may hold values from -25 to 25
- keys: bfloat16 [16384, 1024], P(('dp', 'ctx'), 'tp'), parts along dimension 0, may hold values from -6 to 6
- values: bfloat16 [16384, 1024], P(('dp', 'ctx'), 'tp'), parts along dimension 0, may hold values from -6 to 6
- counts: int32 [128, 32], P('dp'), parts along dimension 0, may hold values from 0 to 8, as said below
- doc_lengths: int32 [64], P('dp'), parts along dimension 0, may hold values from 1 to 2048, 4096 in all
Outputs:
- attended: bfloat16 [16384, 4096], P(('dp', 'ctx'), 'tp'), parts along dimension 0
The draws below stay inside these ranges and needn't reach their ends.
There are 4 independent parts, one for each index of `dp`. The reference program is written for one: setup_inputs(seed, part) draws one part's arguments, and reference() takes and returns one part's arrays. A program takes and returns all parts, laid end to end along the dimension named above; each array names one. Nothing has to cross between parts.
Inputs may be any that keep to these rules, and one draw needn't show every extreme that they name: Every row and every column of counts sums to 128; no entry exceeds 8, and some entry equals 8.
All inputs are finite; a program needn't handle non-finite values.
Results may differ from the reference program's by a relative error of at most 0.006.
Values may be sent and summed in bfloat16 or wider, within the bound.
No kernel may reach another device: no remote copies, remote signals or barrier semaphores. Data moves between devices by JAX's collectives and lax.ppermute only.
A program may use at most 32 MiB of HBM per device.

```python
import math
import jax
import jax.numpy as jnp
import numpy as np
from jax import lax

HQ = 32
KVH = 8
HD = 128
TOK_DEV = 128
DOCS = 16
SEQ = 4096
HALF = 64
N_CTX = 32


def draw_queries(key, part):
    base = jnp.clip(jax.random.normal(jax.random.fold_in(key, 1), (SEQ, HQ, HD), jnp.float32), -6.0, 6.0)
    return base.reshape(SEQ, HQ * HD).astype(jnp.bfloat16)


def draw_keys(key, part):
    base = jnp.clip(jax.random.normal(jax.random.fold_in(key, 2), (SEQ, KVH, HD), jnp.float32), -6.0, 6.0)
    return base.reshape(SEQ, KVH * HD).astype(jnp.bfloat16)


def draw_counts(key, part):
    mean_rows = TOK_DEV // N_CTX
    wobble = jax.random.randint(jax.random.fold_in(key, 21), (N_CTX,), 0, mean_rows + 1)
    wobble = wobble.at[0].set(mean_rows).at[N_CTX - 1].set(0)
    profile = mean_rows + wobble - jnp.roll(wobble, 1)
    owner_perm = jax.random.permutation(jax.random.fold_in(key, 22), N_CTX)
    loader_perm = jax.random.permutation(jax.random.fold_in(key, 23), N_CTX)
    shift = (owner_perm[None, :] - loader_perm[:, None]) % N_CTX
    return jnp.take(profile, shift).astype(jnp.int32)


def shard_levels(rng, extent, shards, low, top_value):
    factor_of, own = 1.0, jax.random.fold_in(rng, 6)
    for position, blocks in shards:
        draws = jnp.exp(jax.random.uniform(jax.random.fold_in(own, position), (blocks,), jnp.float32, low / len(shards), top_value / len(shards)))
        factor_of = factor_of * jnp.repeat(draws, extent[position] // blocks).reshape([-1 if axis == position else 1 for axis in range(len(extent))])
    return factor_of


def split_up(number_of, total, bound, skew):
    loads = [(1 << 20) // math.isqrt(standing ** skew) + 1 for standing in range(2, number_of + 1)]
    surplus, holding = total - bound - (number_of - 1), [1] * (number_of - 1)
    while surplus > 0:
        candidates = [i for i in range(number_of - 1) if holding[i] < bound]
        pool, left = sum([loads[i] for i in candidates]), surplus
        for i in candidates:
            extra = min(bound - holding[i], max(1, left * loads[i] // pool), surplus)
            holding[i] = holding[i] + extra
            surplus = surplus - extra
    return np.array([bound] + holding)


def ragged_sizes(key, count, total, bound, lean):
    if count == 2:
        one = jax.random.randint(key, (), max(1, total - bound), min(bound, total - 1) + 1)
        return jnp.stack([one, total - one])
    sizes = jnp.asarray(split_up(count, total, bound, lean), jnp.int32)
    couples = (count - 1) // 2
    donor, receiver = sizes[1:1 + 2 * couples:2], sizes[2:2 + 2 * couples:2]
    room = jnp.minimum(donor - 1, bound - receiver)
    shifted = jax.random.randint(jax.random.fold_in(key, 1), (couples,), 0, 1 << 20) % (room + 1)
    sizes = sizes.at[1:1 + 2 * couples:2].set(donor - shifted).at[2:2 + 2 * couples:2].set(receiver + shifted)
    return sizes[jax.random.permutation(jax.random.fold_in(key, 2), count)]


def scatter_about(stream_key, extent, scale, reach, split=(), held_as=jnp.bfloat16):
    array = scale * jax.random.normal(stream_key, extent, jnp.float32)
    if split:
        array = array * shard_levels(stream_key, extent, split, -0.22, 0.18)
    return jnp.clip(array, -reach, reach).astype(held_as)


def setup_inputs(seed: int = 0, part: int = 0) -> dict:
    arg_keys = jax.random.split(jax.random.key(seed), 6)
    own_keys = jax.random.split(jax.random.fold_in(arg_keys[5], part), 6)
    return {
        "queries": draw_queries(jax.random.fold_in(jax.random.fold_in(arg_keys[5], part), 71), part),
        "keys": draw_keys(jax.random.fold_in(jax.random.fold_in(arg_keys[5], part), 71), part),
        "values": scatter_about(own_keys[2], (SEQ, KVH * HD), 1.0, 6.0, ((0, 32), (1, 8))),
        "counts": draw_counts(jax.random.fold_in(jax.random.fold_in(arg_keys[5], part), 71), part),
        "doc_lengths": ragged_sizes(own_keys[4], DOCS, SEQ, SEQ // 2, 2).astype(jnp.int32),
    }


def span_pos(owner, local):
    return jnp.where(local < HALF, owner * HALF + local, (2 * N_CTX - 1 - owner) * HALF + local - HALF).astype(jnp.int32)


def loader_positions(counts):
    counts = counts.astype(jnp.int32)
    ends = jnp.cumsum(counts, axis=1).astype(jnp.int32)
    starts = ends - counts
    before = (jnp.cumsum(counts, axis=0) - counts).astype(jnp.int32)
    rowids = jnp.arange(TOK_DEV, dtype=jnp.int32)
    owner = jnp.sum((ends[:, None, :] <= rowids[None, :, None]).astype(jnp.int32), axis=2).astype(jnp.int32)
    start_sel = jnp.take_along_axis(starts, owner, axis=1)
    pre_sel = jnp.take_along_axis(before, owner, axis=1)
    return span_pos(owner, pre_sel + rowids[None, :] - start_sel)


def reference(queries, keys, values, counts, doc_lengths):
    group = HQ // KVH
    where_to = loader_positions(counts).reshape(-1)
    packed_q = jnp.zeros((SEQ, HQ * HD), jnp.bfloat16).at[where_to].set(queries)
    packed_k = jnp.zeros((SEQ, KVH * HD), jnp.bfloat16).at[where_to].set(keys)
    packed_v = jnp.zeros((SEQ, KVH * HD), jnp.bfloat16).at[where_to].set(values)
    doc_ends = jnp.cumsum(doc_lengths.astype(jnp.int32)).astype(jnp.int32)
    places = jnp.arange(SEQ, dtype=jnp.int32)
    segment = jnp.sum((doc_ends[None, :] <= places[:, None]).astype(jnp.int32), axis=1).astype(jnp.int32)
    key_full = packed_k.reshape(SEQ, KVH, HD).astype(jnp.float32)
    value_full = packed_v.reshape(SEQ, KVH, HD).astype(jnp.float32)
    scale = 1.0 / (HD ** 0.5)
    block = 128

    def one_block(index):
        first = (index * block).astype(jnp.int32)
        query_rows = lax.dynamic_slice_in_dim(packed_q, first, block, 0)
        query_rows = query_rows.reshape(block, KVH, group, HD).astype(jnp.float32)
        qpos = first + jnp.arange(block, dtype=jnp.int32)
        qseg = lax.dynamic_slice_in_dim(segment, first, block, 0)
        visible = (places[None, :] <= qpos[:, None]) & (segment[None, :] == qseg[:, None])
        scores = jnp.einsum("qcgd,kcd->cgqk", query_rows, key_full) * scale
        masked = jnp.where(visible, scores, -1e30)
        top = jnp.max(masked, axis=-1, keepdims=True)
        expo = jnp.where(visible, jnp.exp(masked - top), 0.0)
        total = jnp.sum(expo, axis=-1)
        weights = expo.astype(jnp.bfloat16).astype(jnp.float32)
        mixed = jnp.einsum("cgqk,kcd->cgqd", weights, value_full) / total[..., None]
        return jnp.transpose(mixed, (2, 0, 1, 3)).reshape(block, HQ * HD).astype(jnp.bfloat16)

    packed_out = lax.map(one_block, jnp.arange(SEQ // block, dtype=jnp.int32)).reshape(SEQ, HQ * HD)
    owners = jnp.arange(N_CTX, dtype=jnp.int32)[:, None]
    locals_ = jnp.arange(TOK_DEV, dtype=jnp.int32)[None, :]
    own_index = span_pos(owners + 0 * locals_, locals_ + 0 * owners).reshape(-1)
    return jnp.take(packed_out, own_index, axis=0)
```

```python
import jax
import jax.numpy as jnp
from jax import lax
from jax.experimental import pallas as pl
from jax.experimental.pallas import tpu as pltpu
from jax.sharding import PartitionSpec as P

HQ = 32
KVH = 8
HD = 128
GROUP = HQ // KVH
TOK = 128
HALF = 64
NCX = 32
SLOT = 8
SEQ = NCX * TOK
BLOCK = 256
LOG2E = 1.4426950408889634

f32 = jnp.float32
bf16 = jnp.bfloat16
i32 = jnp.int32


def iota(shape, dim):
    return lax.broadcasted_iota(i32, shape, dim)


def pack_kernel(counts_ref, q_ref, out_ref):
    me = lax.axis_index("ctx")
    row = counts_ref[pl.ds(me, 1), :].astype(f32)
    slots = NCX * SLOT
    owner_of = iota((slots, NCX), 0) // SLOT
    owner = iota((slots, NCX), 1)
    start = jnp.sum(jnp.where(owner < owner_of, row, 0.0), axis=1, keepdims=True)
    count = jnp.sum(jnp.where(owner == owner_of, row, 0.0), axis=1, keepdims=True)
    j = (iota((slots, 1), 0) % SLOT).astype(f32)
    want = jnp.where(j < count, start + j, -1.0)
    pick = jnp.where(iota((slots, TOK), 1).astype(f32) == want, 1.0, 0.0).astype(bf16)
    out_ref[...] = jnp.dot(pick, q_ref[...], preferred_element_type=f32).astype(bf16)


def place_kernel(counts_ref, pos_ref):
    counts = counts_ref[...].astype(f32)
    a, b = iota((NCX, NCX), 0), iota((NCX, NCX), 1)
    starts = jnp.dot(counts, (a < b).astype(f32), preferred_element_type=f32)
    before = jnp.dot((b < a).astype(f32), counts, preferred_element_type=f32)
    row = iota((NCX, TOK), 1).astype(f32)
    pos = jnp.zeros((NCX, TOK), f32)
    for o in range(NCX):
        j = row - starts[:, o : o + 1]
        local = before[:, o : o + 1] + j
        here = jnp.where(local < HALF, local + o * HALF, local + ((2 * NCX - 1 - o) * HALF - HALF))
        pos = jnp.where((j >= 0) & (j < counts[:, o : o + 1]), here, pos)
    pos_ref[...] = pos


def attend_kernel(docs_ref, counts_ref, pos_ref, q_ref, kv_ref, out_ref, s_ref, top_ref, acc_ref, sum_ref):
    me = lax.axis_index("ctx")
    slots = NCX * SLOT
    counts = counts_ref[...].astype(f32)
    mine = jnp.sum(jnp.where(iota((NCX, NCX), 1) == me, counts, 0.0), axis=1, keepdims=True)
    src_of, src = iota((NCX, slots), 1) // SLOT, iota((NCX, slots), 0)
    before = jnp.sum(jnp.where(src < src_of, mine, 0.0), axis=0, keepdims=True)
    count = jnp.sum(jnp.where(src == src_of, mine, 0.0), axis=0, keepdims=True)
    j = (iota((1, slots), 1) % SLOT).astype(f32)
    local = jnp.where(j < count, before + j, -1.0)
    pick = jnp.where(iota((TOK, slots), 0).astype(f32) == local, 1.0, 0.0).astype(bf16)
    query = jnp.dot(pick, q_ref[...], preferred_element_type=f32).astype(bf16)

    q_id = iota((TOK, HD), 0)
    q_pos = jnp.where(q_id < HALF, me * HALF + q_id, (2 * NCX - 1 - me) * HALF + q_id - HALF)
    q_first = jnp.zeros((TOK, HD), i32)
    end = jnp.int32(0)
    for d in range(docs_ref.shape[0]):
        end = end + docs_ref[d]
        q_first = jnp.where(q_pos >= end, end, q_first)
    q_pos, q_first = q_pos.astype(f32), q_first.astype(f32)

    per = BLOCK // TOK
    top_ref[...] = jnp.full(top_ref.shape, -1e30, f32)
    for blk in range(SEQ // BLOCK):
        keys = kv_ref[blk * BLOCK : (blk + 1) * BLOCK, :HD]
        seen = []
        for c in range(per):
            k_pos = pos_ref[blk * per + c : blk * per + c + 1, :]
            seen.append((k_pos <= q_pos) & (k_pos >= q_first))
        for h in range(GROUP):
            s = lax.dot_general(
                query[:, h * HD : (h + 1) * HD], keys, (((1,), (1,)), ((), ())), preferred_element_type=f32
            )
            top = top_ref[h]
            for c in range(per):
                part = jnp.where(seen[c], s[:, c * TOK : (c + 1) * TOK], -1e30)
                s_ref[h, :, blk * BLOCK + c * TOK : blk * BLOCK + (c + 1) * TOK] = part
                top = jnp.maximum(top, part)
            top_ref[h] = top
    for h in range(GROUP):
        top_ref[h] = jnp.broadcast_to(jnp.max(top_ref[h], axis=1, keepdims=True), (TOK, HD))
    c2 = LOG2E / HD**0.5
    acc_ref[...] = jnp.zeros(acc_ref.shape, f32)
    sum_ref[...] = jnp.zeros(sum_ref.shape, f32)
    for blk in range(SEQ // BLOCK):
        vals = kv_ref[blk * BLOCK : (blk + 1) * BLOCK, HD:]
        for h in range(GROUP):
            top = top_ref[h]
            total = sum_ref[h]
            weights = []
            for c in range(per):
                part = s_ref[h, :, blk * BLOCK + c * TOK : blk * BLOCK + (c + 1) * TOK]
                e = jnp.exp2((part - top) * c2)
                total = total + e
                weights.append(e.astype(bf16))
            sum_ref[h] = total
            acc_ref[h] += jnp.dot(jnp.concatenate(weights, axis=1), vals, preferred_element_type=f32)
    for h in range(GROUP):
        total = jnp.sum(sum_ref[h], axis=1, keepdims=True)
        out_ref[:, h * HD : (h + 1) * HD] = (acc_ref[h] / total).astype(bf16)


VMEM = pl.BlockSpec(memory_space=pltpu.VMEM)
SMEM = pl.BlockSpec(memory_space=pltpu.SMEM)


def body(queries, keys, values, counts, doc_lengths):
    slots = NCX * SLOT
    packed = pl.pallas_call(
        pack_kernel,
        out_shape=jax.ShapeDtypeStruct((slots, GROUP * HD), bf16),
        in_specs=[VMEM, VMEM],
        out_specs=VMEM,
        name="pack",
    )(counts, queries)
    got = lax.all_to_all(
        packed.reshape(NCX, SLOT, GROUP * HD), "ctx", split_axis=0, concat_axis=0, tiled=True
    ).reshape(slots, GROUP * HD)
    key_value = lax.all_gather(jnp.concatenate([keys, values], axis=1), "ctx", axis=0, tiled=True)
    pos = pl.pallas_call(
        place_kernel,
        out_shape=jax.ShapeDtypeStruct((NCX, TOK), f32),
        in_specs=[VMEM],
        out_specs=VMEM,
        name="place",
    )(counts)
    return pl.pallas_call(
        attend_kernel,
        out_shape=jax.ShapeDtypeStruct((TOK, GROUP * HD), bf16),
        in_specs=[SMEM, VMEM, VMEM, VMEM, VMEM],
        out_specs=VMEM,
        scratch_shapes=[
            pltpu.VMEM((GROUP, TOK, SEQ), f32),
            pltpu.VMEM((GROUP, TOK, HD), f32),
            pltpu.VMEM((GROUP, TOK, HD), f32),
            pltpu.VMEM((GROUP, TOK, HD), f32),
        ],
        name="attend",
    )(doc_lengths, counts, pos, got, key_value)


def solution(mesh):
    placed = (
        P(("dp", "ctx"), "tp"),
        P(("dp", "ctx"), "tp"),
        P(("dp", "ctx"), "tp"),
        P("dp", None),
        P("dp"),
    )
    return jax.shard_map(
        body, mesh=mesh, in_specs=placed, out_specs=P(("dp", "ctx"), "tp"), check_vma=False
    )
```

```python
import functools

import jax
import jax.numpy as jnp
from jax import lax
from jax.experimental import pallas as pl
from jax.experimental.pallas import tpu as pltpu
from jax.sharding import PartitionSpec as P

HQ = 32
KVH = 8
HD = 128
GROUP = HQ // KVH
TOK = 128
HALF = 64
NCX = 32
SLOT = 8
KEYS = NCX // 2 * TOK
BLOCK = 256
C2 = 1.4426950408889634 / HD**0.5
NEG = -1e30
SIDES = [list(range(0, NCX, 2)), list(range(1, NCX, 2))]

f32 = jnp.float32
bf16 = jnp.bfloat16
i32 = jnp.int32


def iota(shape, dim):
    return lax.broadcasted_iota(i32, shape, dim)


def pack_kernel(counts_ref, q_ref, out_ref):
    me = lax.axis_index("ctx")
    row = counts_ref[pl.ds(me, 1), :].astype(f32)
    slots = NCX * SLOT
    owner_of = iota((slots, NCX), 0) // SLOT
    owner = iota((slots, NCX), 1)
    start = jnp.sum(jnp.where(owner < owner_of, row, 0.0), axis=1, keepdims=True)
    count = jnp.sum(jnp.where(owner == owner_of, row, 0.0), axis=1, keepdims=True)
    j = (iota((slots, 1), 0) % SLOT).astype(f32)
    want = jnp.where(j < count, start + j, -1.0)
    pick = jnp.where(iota((slots, TOK), 1).astype(f32) == want, 1.0, 0.0).astype(bf16)
    out_ref[...] = jnp.dot(pick, q_ref[...], preferred_element_type=f32).astype(bf16)


def place_kernel(counts_ref, pos_ref):
    counts = counts_ref[...].astype(f32)
    a, b = iota((NCX, NCX), 0), iota((NCX, NCX), 1)
    starts = jnp.dot(counts, (a < b).astype(f32), preferred_element_type=f32)
    before = jnp.dot((b < a).astype(f32), counts, preferred_element_type=f32)
    row = iota((NCX, TOK), 1).astype(f32)
    pos = jnp.zeros((NCX, TOK), f32)
    for o in range(NCX):
        j = row - starts[:, o : o + 1]
        local = before[:, o : o + 1] + j
        here = jnp.where(local < HALF, local + o * HALF, local + ((2 * NCX - 1 - o) * HALF - HALF))
        pos = jnp.where((j >= 0) & (j < counts[:, o : o + 1]), here, pos)
    pos_ref[...] = pos


def unpack_kernel(counts_ref, got_ref, out_ref):
    me = lax.axis_index("ctx")
    slots = NCX * SLOT
    counts = counts_ref[...].astype(f32)
    mine = jnp.sum(jnp.where(iota((NCX, NCX), 1) == me, counts, 0.0), axis=1, keepdims=True)
    src_of, src = iota((NCX, slots), 1) // SLOT, iota((NCX, slots), 0)
    before = jnp.sum(jnp.where(src < src_of, mine, 0.0), axis=0, keepdims=True)
    count = jnp.sum(jnp.where(src == src_of, mine, 0.0), axis=0, keepdims=True)
    j = (iota((1, slots), 1) % SLOT).astype(f32)
    local = jnp.where(j < count, before + j, -1.0)
    pick = jnp.where(iota((TOK, slots), 0).astype(f32) == local, 1.0, 0.0).astype(bf16)
    out_ref[...] = jnp.dot(pick, got_ref[...], preferred_element_type=f32).astype(bf16)


def attend_kernel(flip, docs_ref, pos_ref, q_ref, kv_ref, out_ref, s_ref, top_ref, acc_ref, sum_ref):
    me = lax.axis_index("ctx")
    parity = me % 2
    owner = me + flip * (1 - 2 * parity)
    q_id = iota((TOK, HD), 0)
    q_pos = jnp.where(q_id < HALF, owner * HALF + q_id, (2 * NCX - 1 - owner) * HALF + q_id - HALF)
    q_first = jnp.zeros((TOK, HD), i32)
    end = jnp.int32(0)
    for d in range(docs_ref.shape[0]):
        end = end + docs_ref[d]
        q_first = jnp.where(q_pos >= end, end, q_first)
    q_pos, q_first = q_pos.astype(f32), q_first.astype(f32)

    per = BLOCK // TOK
    top_ref[...] = jnp.full(top_ref.shape, NEG, f32)
    for blk in range(KEYS // BLOCK):
        keys = kv_ref[blk * BLOCK : (blk + 1) * BLOCK, :HD]
        seen = []
        for c in range(per):
            k_pos = pos_ref[pl.ds(2 * (blk * per + c) + parity, 1), :]
            seen.append((k_pos <= q_pos) & (k_pos >= q_first))
        for h in range(GROUP):
            s = lax.dot_general(
                q_ref[:, h * HD : (h + 1) * HD], keys, (((1,), (1,)), ((), ())), preferred_element_type=f32
            )
            top = top_ref[h]
            for c in range(per):
                part = jnp.where(seen[c], s[:, c * TOK : (c + 1) * TOK], NEG)
                s_ref[h, :, blk * BLOCK + c * TOK : blk * BLOCK + (c + 1) * TOK] = part
                top = jnp.maximum(top, part)
            top_ref[h] = top
    for h in range(GROUP):
        top_ref[h] = jnp.broadcast_to(jnp.max(top_ref[h], axis=1, keepdims=True), (TOK, HD))
    acc_ref[...] = jnp.zeros(acc_ref.shape, f32)
    sum_ref[...] = jnp.zeros(sum_ref.shape, f32)
    for blk in range(KEYS // BLOCK):
        vals = kv_ref[blk * BLOCK : (blk + 1) * BLOCK, HD:]
        for h in range(GROUP):
            top = top_ref[h]
            total = sum_ref[h]
            weights = []
            for c in range(per):
                part = s_ref[h, :, blk * BLOCK + c * TOK : blk * BLOCK + (c + 1) * TOK]
                e = jnp.exp2((part - top) * C2)
                total = total + e
                weights.append(e.astype(bf16))
            sum_ref[h] = total
            acc_ref[h] += jnp.dot(jnp.concatenate(weights, axis=1), vals, preferred_element_type=f32)
    lane = iota((TOK, HD), 1)
    stats = jnp.zeros((TOK, HD), f32)
    for h in range(GROUP):
        out_ref[:, h * HD : (h + 1) * HD] = acc_ref[h]
        stats = jnp.where(lane == h, top_ref[h], stats)
        stats = jnp.where(lane == GROUP + h, jnp.sum(sum_ref[h], axis=1, keepdims=True), stats)
    out_ref[:, GROUP * HD :] = stats


def join_kernel(a_ref, b_ref, out_ref):
    sa, sb = a_ref[:, GROUP * HD :], b_ref[:, GROUP * HD :]
    for h in range(GROUP):
        top_a, top_b = sa[:, h : h + 1], sb[:, h : h + 1]
        top = jnp.maximum(top_a, top_b)
        wa, wb = jnp.exp2((top_a - top) * C2), jnp.exp2((top_b - top) * C2)
        total = sa[:, GROUP + h : GROUP + h + 1] * wa + sb[:, GROUP + h : GROUP + h + 1] * wb
        wa, wb = wa / total, wb / total
        cols = slice(h * HD, (h + 1) * HD)
        out_ref[:, cols] = (a_ref[:, cols] * wa + b_ref[:, cols] * wb).astype(bf16)


VMEM = pl.BlockSpec(memory_space=pltpu.VMEM)
SMEM = pl.BlockSpec(memory_space=pltpu.SMEM)


def swap(x):
    return lax.ppermute(x, "ctx", [(i, i ^ 1) for i in range(NCX)])


def attend(flip, doc_lengths, pos, query, key_value):
    return pl.pallas_call(
        functools.partial(attend_kernel, flip),
        out_shape=jax.ShapeDtypeStruct((TOK, GROUP * HD + HD), f32),
        in_specs=[SMEM, VMEM, VMEM, VMEM],
        out_specs=VMEM,
        scratch_shapes=[
            pltpu.VMEM((GROUP, TOK, KEYS), f32),
            pltpu.VMEM((GROUP, TOK, HD), f32),
            pltpu.VMEM((GROUP, TOK, HD), f32),
            pltpu.VMEM((GROUP, TOK, HD), f32),
        ],
        cost_estimate=pl.CostEstimate(
            flops=4 * GROUP * TOK * KEYS * HD, bytes_accessed=2 * KEYS * HD * 2, transcendentals=GROUP * TOK * KEYS
        ),
        name="attend_partner" if flip else "attend_own",
    )(doc_lengths, pos, query, key_value)


def body(queries, keys, values, counts, doc_lengths):
    slots = NCX * SLOT
    wide = GROUP * HD
    key_value = jnp.concatenate([keys, values], axis=1)
    key_value, queries = lax.optimization_barrier((key_value, queries))
    packed = pl.pallas_call(
        pack_kernel,
        out_shape=jax.ShapeDtypeStruct((slots, wide), bf16),
        in_specs=[VMEM, VMEM],
        out_specs=VMEM,
        name="pack",
    )(counts, queries)
    got = lax.all_to_all(
        packed.reshape(NCX, SLOT, wide), "ctx", split_axis=0, concat_axis=0, tiled=True
    ).reshape(slots, wide)
    key_value = lax.all_gather(key_value, "ctx", axis=0, tiled=True, axis_index_groups=SIDES)
    pos = pl.pallas_call(
        place_kernel,
        out_shape=jax.ShapeDtypeStruct((NCX, TOK), f32),
        in_specs=[VMEM],
        out_specs=VMEM,
        name="place",
    )(counts)
    query = pl.pallas_call(
        unpack_kernel,
        out_shape=jax.ShapeDtypeStruct((TOK, wide), bf16),
        in_specs=[VMEM, VMEM],
        out_specs=VMEM,
        name="unpack",
    )(counts, got)
    partner = attend(1, doc_lengths, pos, swap(query), key_value)
    other = swap(partner)
    own = attend(0, doc_lengths, pos, query, key_value)
    return pl.pallas_call(
        join_kernel,
        out_shape=jax.ShapeDtypeStruct((TOK, wide), bf16),
        in_specs=[VMEM, VMEM],
        out_specs=VMEM,
        name="join",
    )(own, other)


def solution(mesh):
    placed = (
        P(("dp", "ctx"), "tp"),
        P(("dp", "ctx"), "tp"),
        P(("dp", "ctx"), "tp"),
        P("dp", None),
        P("dp"),
    )
    return jax.shard_map(
        body, mesh=mesh, in_specs=placed, out_specs=P(("dp", "ctx"), "tp"), check_vma=False
    )
```

```python
import functools

import jax
import jax.numpy as jnp
from jax import lax
from jax.experimental import pallas as pl
from jax.experimental.pallas import tpu as pltpu
from jax.sharding import PartitionSpec as P

HQ = 32
KVH = 8
HD = 128
GROUP = HQ // KVH
TOK = 128
HALF = 64
NCX = 32
SLOT = 8
KEYS = NCX // 2 * TOK
MAIN = 124
REST = TOK - MAIN
C2 = 1.4426950408889634 / HD**0.5
NEG = -1e30
SIDES = [list(range(0, NCX, 2)), list(range(1, NCX, 2))]

f32 = jnp.float32
bf16 = jnp.bfloat16
i32 = jnp.int32


def iota(shape, dim):
    return lax.broadcasted_iota(i32, shape, dim)


def pack_kernel(counts_ref, q_ref, k_ref, v_ref, out_ref, kv_ref):
    me = lax.axis_index("ctx")
    row = counts_ref[pl.ds(me, 1), :].astype(f32)
    slots = NCX * SLOT
    owner_of = iota((slots, NCX), 0) // SLOT
    owner = iota((slots, NCX), 1)
    start = jnp.sum(jnp.where(owner < owner_of, row, 0.0), axis=1, keepdims=True)
    count = jnp.sum(jnp.where(owner == owner_of, row, 0.0), axis=1, keepdims=True)
    j = iota((slots, 1), 0) % SLOT
    jf = j.astype(f32)
    want = jnp.where(jf < count, start + jf, -1.0)
    lane = iota((slots, TOK), 1)
    pick = jnp.where(lane.astype(f32) == want, 1.0, 0.0).astype(bf16)
    wide = GROUP * HD
    out_ref[:, :wide] = jnp.dot(pick, q_ref[...], preferred_element_type=f32).astype(bf16)
    pick_k = jnp.where(lane == jnp.where(j < REST, MAIN + j, -1), 1.0, 0.0).astype(bf16)
    pick_v = jnp.where(lane == jnp.where(j >= REST, MAIN + j - REST, -1), 1.0, 0.0).astype(bf16)
    rest = jnp.dot(pick_k, k_ref[...], preferred_element_type=f32)
    rest = rest + jnp.dot(pick_v, v_ref[...], preferred_element_type=f32)
    out_ref[:, wide:] = rest.astype(bf16)
    kv_ref[:, :HD] = k_ref[:MAIN, :]
    kv_ref[:, HD:] = v_ref[:MAIN, :]


def place_kernel(counts_ref, pos_ref):
    counts = counts_ref[...].astype(f32)
    a, b = iota((NCX, NCX), 0), iota((NCX, NCX), 1)
    starts = jnp.dot(counts, (a < b).astype(f32), preferred_element_type=f32)
    before = jnp.dot((b < a).astype(f32), counts, preferred_element_type=f32)
    row = iota((NCX, TOK), 1).astype(f32)
    pos = jnp.zeros((NCX, TOK), f32)
    for o in range(NCX):
        j = row - starts[:, o : o + 1]
        local = before[:, o : o + 1] + j
        here = jnp.where(local < HALF, local + o * HALF, local + ((2 * NCX - 1 - o) * HALF - HALF))
        pos = jnp.where((j >= 0) & (j < counts[:, o : o + 1]), here, pos)
    pos_ref[:NCX, :] = pos
    parity = lax.axis_index("ctx") % 2
    loader, lane = iota((NCX, TOK), 0), iota((NCX, TOK), 1)
    rest = jnp.zeros((NCX, TOK), f32)
    for r in range(REST):
        here = (loader == 2 * (lane // REST) + parity) & (lane % REST == r)
        rest = jnp.where(here, pos[:, MAIN + r : MAIN + r + 1], rest)
    pos_ref[NCX:, :] = jnp.broadcast_to(jnp.sum(rest, axis=0, keepdims=True), (8, TOK))


def unpack_kernel(counts_ref, got_ref, out_ref, rest_ref):
    me = lax.axis_index("ctx")
    slots = NCX * SLOT
    counts = counts_ref[...].astype(f32)
    mine = jnp.sum(jnp.where(iota((NCX, NCX), 1) == me, counts, 0.0), axis=1, keepdims=True)
    src_of, src = iota((NCX, slots), 1) // SLOT, iota((NCX, slots), 0)
    before = jnp.sum(jnp.where(src < src_of, mine, 0.0), axis=0, keepdims=True)
    count = jnp.sum(jnp.where(src == src_of, mine, 0.0), axis=0, keepdims=True)
    j = (iota((1, slots), 1) % SLOT).astype(f32)
    local = jnp.where(j < count, before + j, -1.0)
    pick = jnp.where(iota((TOK, slots), 0).astype(f32) == local, 1.0, 0.0).astype(bf16)
    wide = GROUP * HD
    out_ref[...] = jnp.dot(pick, got_ref[:, :wide], preferred_element_type=f32).astype(bf16)
    n = NCX // 2 * REST
    row, slot = iota((n, slots), 0), iota((n, slots), 1)
    at = (2 * (row // REST) + me % 2) * SLOT + row % REST
    for c in range(2):
        pick = jnp.where(slot == at + c * REST, 1.0, 0.0).astype(bf16)
        rest = jnp.dot(pick, got_ref[:, wide:], preferred_element_type=f32)
        rest_ref[:, c * HD : (c + 1) * HD] = rest.astype(bf16)


def attend_kernel(flip, docs_ref, pos_ref, q_ref, kv_ref, rest_ref, out_ref, s_ref, top_ref, acc_ref, sum_ref):
    me = lax.axis_index("ctx")
    parity = me % 2
    owner = me + flip * (1 - 2 * parity)
    q_id = iota((TOK, HD), 0)
    q_pos = jnp.where(q_id < HALF, owner * HALF + q_id, (2 * NCX - 1 - owner) * HALF + q_id - HALF)
    q_first = jnp.zeros((TOK, HD), i32)
    end = jnp.int32(0)
    for d in range(docs_ref.shape[0]):
        end = end + docs_ref[d]
        q_first = jnp.where(q_pos >= end, end, q_first)
    q_pos, q_first = q_pos.astype(f32), q_first.astype(f32)

    blocks = [(i, MAIN) for i in range(NCX // 2)] + [(NCX // 2, NCX // 2 * REST)]

    def rows(i, cols):
        return kv_ref[i, :, cols] if i < NCX // 2 else rest_ref[:, cols]

    top_ref[...] = jnp.full(top_ref.shape, NEG, f32)
    for i, n in blocks:
        keys = rows(i, slice(0, HD))
        k_pos = pos_ref[pl.ds(2 * i + parity, 1), :] if i < NCX // 2 else pos_ref[NCX : NCX + 1, :]
        seen = ((k_pos <= q_pos) & (k_pos >= q_first))[:, :n]
        for h in range(GROUP):
            s = lax.dot_general(
                q_ref[:, h * HD : (h + 1) * HD], keys, (((1,), (1,)), ((), ())), preferred_element_type=f32
            )
            part = jnp.where(seen, s, NEG)
            s_ref[h, :, i * TOK : i * TOK + n] = part
            top_ref[h, :, :n] = jnp.maximum(top_ref[h, :, :n], part)
    for h in range(GROUP):
        top_ref[h] = jnp.broadcast_to(jnp.max(top_ref[h], axis=1, keepdims=True), (TOK, HD))
    acc_ref[...] = jnp.zeros(acc_ref.shape, f32)
    sum_ref[...] = jnp.zeros(sum_ref.shape, f32)
    for i, n in blocks:
        vals = rows(i, slice(HD, 2 * HD))
        for h in range(GROUP):
            e = jnp.exp2((s_ref[h, :, i * TOK : i * TOK + n] - top_ref[h, :, :n]) * C2)
            sum_ref[h, :, :n] += e
            acc_ref[h] += jnp.dot(e.astype(bf16), vals, preferred_element_type=f32)
    lane = iota((TOK, HD), 1)
    stats = jnp.zeros((TOK, HD), f32)
    for h in range(GROUP):
        out_ref[:, h * HD : (h + 1) * HD] = acc_ref[h]
        stats = jnp.where(lane == h, top_ref[h], stats)
        stats = jnp.where(lane == GROUP + h, jnp.sum(sum_ref[h], axis=1, keepdims=True), stats)
    out_ref[:, GROUP * HD :] = stats


def join_kernel(a_ref, b_ref, out_ref):
    sa, sb = a_ref[:, GROUP * HD :], b_ref[:, GROUP * HD :]
    for h in range(GROUP):
        top_a, top_b = sa[:, h : h + 1], sb[:, h : h + 1]
        top = jnp.maximum(top_a, top_b)
        wa, wb = jnp.exp2((top_a - top) * C2), jnp.exp2((top_b - top) * C2)
        total = sa[:, GROUP + h : GROUP + h + 1] * wa + sb[:, GROUP + h : GROUP + h + 1] * wb
        wa, wb = wa / total, wb / total
        cols = slice(h * HD, (h + 1) * HD)
        out_ref[:, cols] = (a_ref[:, cols] * wa + b_ref[:, cols] * wb).astype(bf16)


VMEM = pl.BlockSpec(memory_space=pltpu.VMEM)
SMEM = pl.BlockSpec(memory_space=pltpu.SMEM)


def swap(x):
    return lax.ppermute(x, "ctx", [(i, i ^ 1) for i in range(NCX)])


def attend(flip, doc_lengths, pos, query, key_value, rest):
    return pl.pallas_call(
        functools.partial(attend_kernel, flip),
        out_shape=jax.ShapeDtypeStruct((TOK, GROUP * HD + HD), f32),
        in_specs=[SMEM, VMEM, VMEM, VMEM, VMEM],
        out_specs=VMEM,
        scratch_shapes=[
            pltpu.VMEM((GROUP, TOK, KEYS + TOK), f32),
            pltpu.VMEM((GROUP, TOK, HD), f32),
            pltpu.VMEM((GROUP, TOK, HD), f32),
            pltpu.VMEM((GROUP, TOK, HD), f32),
        ],
        cost_estimate=pl.CostEstimate(
            flops=4 * GROUP * TOK * KEYS * HD, bytes_accessed=2 * KEYS * HD * 2, transcendentals=GROUP * TOK * KEYS
        ),
        name="attend_partner" if flip else "attend_own",
    )(doc_lengths, pos, query, key_value, rest)


def body(queries, keys, values, counts, doc_lengths):
    slots = NCX * SLOT
    wide = GROUP * HD
    packed, key_value = pl.pallas_call(
        pack_kernel,
        out_shape=(
            jax.ShapeDtypeStruct((slots, wide + HD), bf16),
            jax.ShapeDtypeStruct((MAIN, 2 * HD), bf16),
        ),
        in_specs=[VMEM, VMEM, VMEM, VMEM],
        out_specs=(VMEM, VMEM),
        name="pack",
    )(counts, queries, keys, values)
    got = lax.all_to_all(
        packed.reshape(NCX, SLOT, wide + HD), "ctx", split_axis=0, concat_axis=0, tiled=True
    )
    key_value = lax.all_gather(key_value, "ctx", axis=0, axis_index_groups=SIDES)
    got, key_value = lax.optimization_barrier((got, key_value))
    got = got.reshape(slots, wide + HD)
    pos = pl.pallas_call(
        place_kernel,
        out_shape=jax.ShapeDtypeStruct((NCX + 8, TOK), f32),
        in_specs=[VMEM],
        out_specs=VMEM,
        name="place",
    )(counts)
    query, rest = pl.pallas_call(
        unpack_kernel,
        out_shape=(
            jax.ShapeDtypeStruct((TOK, wide), bf16),
            jax.ShapeDtypeStruct((NCX // 2 * REST, 2 * HD), bf16),
        ),
        in_specs=[VMEM, VMEM],
        out_specs=(VMEM, VMEM),
        name="unpack",
    )(counts, got)
    partner = attend(1, doc_lengths, pos, swap(query), key_value, rest)
    other = swap(partner)
    own = attend(0, doc_lengths, pos, query, key_value, rest)
    return pl.pallas_call(
        join_kernel,
        out_shape=jax.ShapeDtypeStruct((TOK, wide), bf16),
        in_specs=[VMEM, VMEM],
        out_specs=VMEM,
        name="join",
    )(own, other)


def solution(mesh):
    placed = (
        P(("dp", "ctx"), "tp"),
        P(("dp", "ctx"), "tp"),
        P(("dp", "ctx"), "tp"),
        P("dp", None),
        P("dp"),
    )
    return jax.shard_map(
        body, mesh=mesh, in_specs=placed, out_specs=P(("dp", "ctx"), "tp"), check_vma=False
    )
```

```python
import functools

import jax
import jax.numpy as jnp
from jax import lax
from jax.experimental import pallas as pl
from jax.experimental.pallas import tpu as pltpu
from jax.sharding import PartitionSpec as P

HQ = 32
KVH = 8
HD = 128
GROUP = HQ // KVH
TOK = 128
HALF = 64
NCX = 32
SLOT = 8
SIDE = NCX // 2
KEYS = SIDE * TOK
MAIN = 124
REST = TOK - MAIN
C2 = 1.4426950408889634 / HD**0.5
NEG = -1e30
FAR = 1e9
SIDES = [list(range(0, NCX, 2)), list(range(1, NCX, 2))]

f32 = jnp.float32
bf16 = jnp.bfloat16
i32 = jnp.int32


def iota(shape, dim):
    return lax.broadcasted_iota(i32, shape, dim)


def pack_kernel(counts_ref, q_ref, k_ref, v_ref, out_ref, kv_ref):
    me = lax.axis_index("ctx")
    row = counts_ref[pl.ds(me, 1), :].astype(f32)
    slots = NCX * SLOT
    owner_of = iota((slots, NCX), 0) // SLOT
    owner = iota((slots, NCX), 1)
    start = jnp.sum(jnp.where(owner < owner_of, row, 0.0), axis=1, keepdims=True)
    count = jnp.sum(jnp.where(owner == owner_of, row, 0.0), axis=1, keepdims=True)
    j = iota((slots, 1), 0) % SLOT
    jf = j.astype(f32)
    want = jnp.where(jf < count, start + jf, -1.0)
    lane = iota((slots, TOK), 1)
    pick = jnp.where(lane.astype(f32) == want, 1.0, 0.0).astype(bf16)
    wide = GROUP * HD
    out_ref[:, :wide] = jnp.dot(pick, q_ref[...], preferred_element_type=f32).astype(bf16)
    pick_k = jnp.where(lane == jnp.where(j < REST, MAIN + j, -1), 1.0, 0.0).astype(bf16)
    pick_v = jnp.where(lane == jnp.where(j >= REST, MAIN + j - REST, -1), 1.0, 0.0).astype(bf16)
    rest = jnp.dot(pick_k, k_ref[...], preferred_element_type=f32)
    rest = rest + jnp.dot(pick_v, v_ref[...], preferred_element_type=f32)
    out_ref[:, wide:] = rest.astype(bf16)
    kv_ref[:, :HD] = k_ref[:MAIN, :]
    kv_ref[:, HD:] = v_ref[:MAIN, :]


def place_kernel(counts_ref, kv_ref, rest_ref, pos_ref, all_ref):
    parity = lax.axis_index("ctx") % 2
    counts = counts_ref[...].astype(f32)
    a, b = iota((NCX, NCX), 0), iota((NCX, NCX), 1)
    side = (iota((SIDE, NCX), 1) == 2 * iota((SIDE, NCX), 0) + parity).astype(f32)
    sizes = jnp.dot(side, counts, preferred_element_type=f32)
    starts = jnp.dot(sizes, (a < b).astype(f32), preferred_element_type=f32)
    upto = (b[:SIDE] < 2 * a[:SIDE] + parity).astype(f32)
    before = jnp.dot(upto, counts, preferred_element_type=f32)
    row = iota((SIDE, TOK), 1).astype(f32)
    pos = jnp.zeros((SIDE, TOK), f32)
    for o in range(NCX):
        j = row - starts[:, o : o + 1]
        local = before[:, o : o + 1] + j
        here = jnp.where(local < HALF, local + o * HALF, local + ((2 * NCX - 1 - o) * HALF - HALF))
        pos = jnp.where((j >= 0) & (j < sizes[:, o : o + 1]), here, pos)
    loader, lane = iota((SIDE, TOK), 0), iota((SIDE, TOK), 1)
    rest = jnp.zeros((SIDE, TOK), f32)
    for r in range(REST):
        here = (loader == lane // REST) & (lane % REST == r)
        rest = jnp.where(here, pos[:, MAIN + r : MAIN + r + 1], rest)
    pos_ref[:SIDE, :] = jnp.where(lane < MAIN, pos, FAR)
    rest = jnp.where(lane[:1] < SIDE * REST, jnp.sum(rest, axis=0, keepdims=True), FAR)
    pos_ref[SIDE:, :] = jnp.broadcast_to(rest, (8, TOK))
    for i in range(SIDE):
        all_ref[(i + 1) * TOK - 16 : (i + 1) * TOK, :] = jnp.zeros((16, 2 * HD), bf16)
        all_ref[i * TOK : i * TOK + MAIN, :] = kv_ref[i]
    all_ref[SIDE * TOK : SIDE * TOK + SIDE * REST, :] = rest_ref[...]
    all_ref[SIDE * TOK + SIDE * REST :, :] = jnp.zeros((TOK - SIDE * REST, 2 * HD), bf16)


def unpack_kernel(counts_ref, got_ref, out_ref, rest_ref):
    me = lax.axis_index("ctx")
    slots = NCX * SLOT
    counts = counts_ref[...].astype(f32)
    mine = jnp.sum(jnp.where(iota((NCX, NCX), 1) == me, counts, 0.0), axis=1, keepdims=True)
    src_of, src = iota((NCX, slots), 1) // SLOT, iota((NCX, slots), 0)
    before = jnp.sum(jnp.where(src < src_of, mine, 0.0), axis=0, keepdims=True)
    count = jnp.sum(jnp.where(src == src_of, mine, 0.0), axis=0, keepdims=True)
    j = (iota((1, slots), 1) % SLOT).astype(f32)
    local = jnp.where(j < count, before + j, -1.0)
    pick = jnp.where(iota((TOK, slots), 0).astype(f32) == local, 1.0, 0.0).astype(bf16)
    wide = GROUP * HD
    for h in range(GROUP):
        picked = jnp.dot(pick, got_ref[:, h * HD : (h + 1) * HD], preferred_element_type=f32)
        out_ref[h * TOK : (h + 1) * TOK, :] = picked.astype(bf16)
    n = SIDE * REST
    row, slot = iota((n, slots), 0), iota((n, slots), 1)
    at = (2 * (row // REST) + me % 2) * SLOT + row % REST
    for c in range(2):
        pick = jnp.where(slot == at + c * REST, 1.0, 0.0).astype(bf16)
        rest = jnp.dot(pick, got_ref[:, wide:], preferred_element_type=f32)
        rest_ref[:, c * HD : (c + 1) * HD] = rest.astype(bf16)


def attend_kernel(flip, docs_ref, pos_ref, q_ref, kv_ref, out_ref, s_ref, p_ref, bias_ref):
    me = lax.axis_index("ctx")
    owner = me + flip * (1 - 2 * (me % 2))
    q_id = iota((TOK, HD), 0)
    q_pos = jnp.where(q_id < HALF, owner * HALF + q_id, (2 * NCX - 1 - owner) * HALF + q_id - HALF)
    q_first = jnp.zeros((TOK, HD), i32)
    end = jnp.int32(0)
    for d in range(docs_ref.shape[0]):
        end = end + docs_ref[d]
        q_first = jnp.where(q_pos >= end, end, q_first)
    q_pos, q_first = q_pos.astype(f32), q_first.astype(f32)

    tops = [jnp.full((TOK, HD), NEG, f32) for _ in range(GROUP)]
    for i in range(0, SIDE + 1, 2):
        n = min(2, SIDE + 1 - i)
        for c in range(n):
            k_pos = pos_ref[i + c : i + c + 1, :]
            bias_ref[:, c * TOK : (c + 1) * TOK] = jnp.where((k_pos <= q_pos) & (k_pos >= q_first), 0.0, NEG)
        s = lax.dot_general(
            q_ref[...],
            kv_ref[i * TOK : (i + n) * TOK, :HD],
            (((1,), (1,)), ((), ())),
            preferred_element_type=f32,
        )
        for h in range(GROUP):
            for c in range(n):
                cols = slice(c * TOK, (c + 1) * TOK)
                part = s[h * TOK : (h + 1) * TOK, cols] + bias_ref[:, cols]
                s_ref[h * TOK : (h + 1) * TOK, (i + c) * TOK : (i + c + 1) * TOK] = part
                tops[h] = jnp.maximum(tops[h], part)
    lane = iota((TOK, HD), 1)
    stats = jnp.zeros((TOK, HD), f32)
    totals = []
    for h in range(GROUP):
        top = jnp.broadcast_to(jnp.max(tops[h], axis=1, keepdims=True), (TOK, HD))
        total = jnp.zeros((TOK, HD), f32)
        for i in range(SIDE + 1):
            cols = slice(i * TOK, (i + 1) * TOK)
            e = jnp.exp2((s_ref[h * TOK : (h + 1) * TOK, cols] - top) * C2)
            total = total + e
            p_ref[h * TOK : (h + 1) * TOK, cols] = e.astype(bf16)
        total = jnp.broadcast_to(jnp.sum(total, axis=1, keepdims=True), (TOK, HD))
        totals.append(total)
        for k, value in ((h, top), (GROUP + h, total)):
            if flip:
                for term in range(3):
                    piece = value.astype(bf16).astype(f32)
                    stats = jnp.where(lane == term * 2 * GROUP + k, piece, stats)
                    value = value - piece
            else:
                stats = jnp.where(lane == k, value, stats)
    acc = jnp.dot(p_ref[...], kv_ref[:, HD:], preferred_element_type=f32)
    for h in range(GROUP):
        rows = slice(h * TOK, (h + 1) * TOK)
        out_ref[rows, :] = (acc[rows] / totals[h]).astype(bf16) if flip else acc[rows]
    out_ref[GROUP * TOK :, :] = stats.astype(out_ref.dtype)


def join_kernel(a_ref, b_ref, out_ref):
    sa = a_ref[GROUP * TOK :, :]
    sb = b_ref[GROUP * TOK :, :].astype(f32)

    def stat(k):
        return sum(sb[:, term * 2 * GROUP + k : term * 2 * GROUP + k + 1] for term in range(3))

    for h in range(GROUP):
        top_a, top_b = sa[:, h : h + 1], stat(h)
        top = jnp.maximum(top_a, top_b)
        wa = jnp.exp2((top_a - top) * C2)
        wb = jnp.exp2((top_b - top) * C2) * stat(GROUP + h)
        total = sa[:, GROUP + h : GROUP + h + 1] * wa + wb
        wa, wb = wa / total, wb / total
        rows = slice(h * TOK, (h + 1) * TOK)
        out_ref[:, h * HD : (h + 1) * HD] = (a_ref[rows, :] * wa + b_ref[rows, :].astype(f32) * wb).astype(bf16)


VMEM = pl.BlockSpec(memory_space=pltpu.VMEM)
LIMIT = pltpu.CompilerParams(vmem_limit_bytes=24 * 2**20)
SMEM = pl.BlockSpec(memory_space=pltpu.SMEM)


def near(x):
    return pltpu.with_memory_space_constraint(x, pltpu.VMEM)


def swap(x):
    return lax.ppermute(x, "ctx", [(i, i ^ 1) for i in range(NCX)])


def attend(flip, doc_lengths, pos, query, key_value):
    span = KEYS + TOK
    return pl.pallas_call(
        functools.partial(attend_kernel, flip),
        out_shape=pltpu.VMEM((GROUP * TOK + TOK, HD), bf16 if flip else f32),
        in_specs=[SMEM, VMEM, VMEM, VMEM],
        out_specs=VMEM,
        scratch_shapes=[
            pltpu.VMEM((GROUP * TOK, span), f32),
            pltpu.VMEM((GROUP * TOK, span), bf16),
            pltpu.VMEM((TOK, 2 * TOK), f32),
        ],
        cost_estimate=pl.CostEstimate(
            flops=4 * GROUP * TOK * KEYS * HD, bytes_accessed=2 * KEYS * HD * 2, transcendentals=GROUP * TOK * KEYS
        ),
        compiler_params=LIMIT,
        name="attend_partner" if flip else "attend_own",
    )(doc_lengths, pos, query, key_value)


def body(queries, keys, values, counts, doc_lengths):
    slots = NCX * SLOT
    wide = GROUP * HD
    packed, key_value = pl.pallas_call(
        pack_kernel,
        out_shape=(
            pltpu.VMEM((slots, wide + HD), bf16),
            pltpu.VMEM((MAIN, 2 * HD), bf16),
        ),
        in_specs=[VMEM, VMEM, VMEM, VMEM],
        out_specs=(VMEM, VMEM),
        compiler_params=LIMIT,
        name="pack",
    )(counts, queries, keys, values)
    got = lax.all_to_all(
        packed.reshape(NCX, SLOT, wide + HD), "ctx", split_axis=0, concat_axis=0, tiled=True
    )
    key_value = lax.all_gather(key_value, "ctx", axis=0, axis_index_groups=SIDES)
    got, key_value = lax.optimization_barrier((got, key_value))
    query, rest = pl.pallas_call(
        unpack_kernel,
        out_shape=(
            pltpu.VMEM((GROUP * TOK, HD), bf16),
            pltpu.VMEM((SIDE * REST, 2 * HD), bf16),
        ),
        in_specs=[VMEM, VMEM],
        out_specs=(VMEM, VMEM),
        compiler_params=LIMIT,
        name="unpack",
    )(counts, near(got.reshape(slots, wide + HD)))
    pos, key_value = pl.pallas_call(
        place_kernel,
        out_shape=(
            pltpu.VMEM((SIDE + 8, TOK), f32),
            pltpu.VMEM((KEYS + TOK, 2 * HD), bf16),
        ),
        in_specs=[VMEM, VMEM, VMEM],
        out_specs=(VMEM, VMEM),
        compiler_params=LIMIT,
        name="place",
    )(counts, near(key_value), near(rest))
    pos, query, key_value = near(pos), near(query), near(key_value)
    partner = attend(1, doc_lengths, pos, near(swap(query)), key_value)
    other = swap(partner)
    own = attend(0, doc_lengths, pos, query, key_value)
    return pl.pallas_call(
        join_kernel,
        out_shape=jax.ShapeDtypeStruct((TOK, wide), bf16),
        in_specs=[VMEM, VMEM],
        out_specs=VMEM,
        compiler_params=LIMIT,
        name="join",
    )(near(own), near(other))


def solution(mesh):
    placed = (
        P(("dp", "ctx"), "tp"),
        P(("dp", "ctx"), "tp"),
        P(("dp", "ctx"), "tp"),
        P("dp", None),
        P("dp"),
    )
    return jax.shard_map(
        body, mesh=mesh, in_specs=placed, out_specs=P(("dp", "ctx"), "tp"), check_vma=False
    )
```

```python
import functools

import jax
import jax.numpy as jnp
from jax import lax
from jax.experimental import pallas as pl
from jax.experimental.pallas import tpu as pltpu
from jax.sharding import PartitionSpec as P

HQ = 32
KVH = 8
HD = 128
GROUP = HQ // KVH
TOK = 128
HALF = 64
NCX = 32
SLOT = 8
SIDE = NCX // 2
KEYS = SIDE * TOK
MAIN = 127
REST = TOK - MAIN
PARTS = 2
SPAN = SLOT // PARTS * GROUP * HD + HD
C2 = 1.4426950408889634 / HD**0.5
NEG = -1e30
FAR = 1e9
SIDES = [list(range(0, NCX, 2)), list(range(1, NCX, 2))]

f32 = jnp.float32
bf16 = jnp.bfloat16
i32 = jnp.int32


def iota(shape, dim):
    return lax.broadcasted_iota(i32, shape, dim)


def pack_kernel(counts_ref, q_ref, k_ref, v_ref, out_ref, kv_ref):
    me = lax.axis_index("ctx")
    row = counts_ref[pl.ds(me, 1), :].astype(f32)
    n = NCX * PARTS
    owner_of, owner = iota((n, NCX), 0) // PARTS, iota((n, NCX), 1)
    start = jnp.sum(jnp.where(owner < owner_of, row, 0.0), axis=1, keepdims=True)
    count = jnp.sum(jnp.where(owner == owner_of, row, 0.0), axis=1, keepdims=True)
    part = iota((n, 1), 0) % PARTS
    lane = iota((n, TOK), 1).astype(f32)
    pieces = []
    for c in range(SLOT // PARTS):
        j = (part * (SLOT // PARTS) + c).astype(f32)
        pick = jnp.where(lane == jnp.where(j < count, start + j, -1.0), 1.0, 0.0).astype(bf16)
        pieces.append(jnp.dot(pick, q_ref[...], preferred_element_type=f32).astype(bf16))
    last = jnp.where(part == 0, k_ref[MAIN:, :].astype(f32), v_ref[MAIN:, :].astype(f32))
    pieces.append(last.astype(bf16))
    out_ref[...] = jnp.concatenate(pieces, axis=1).reshape(NCX, PARTS, SPAN)
    kv_ref[:, :HD] = k_ref[:MAIN, :]
    kv_ref[:, HD:] = v_ref[:MAIN, :]


def place_kernel(counts_ref, kv_ref, rest_ref, pos_ref, all_ref):
    parity = lax.axis_index("ctx") % 2
    counts = counts_ref[...].astype(f32)
    a, b = iota((NCX, NCX), 0), iota((NCX, NCX), 1)
    side = (iota((SIDE, NCX), 1) == 2 * iota((SIDE, NCX), 0) + parity).astype(f32)
    sizes = jnp.dot(side, counts, preferred_element_type=f32)
    starts = jnp.dot(sizes, (a < b).astype(f32), preferred_element_type=f32)
    upto = (b[:SIDE] < 2 * a[:SIDE] + parity).astype(f32)
    before = jnp.dot(upto, counts, preferred_element_type=f32)
    row = iota((SIDE, TOK), 1).astype(f32)
    pos = jnp.zeros((SIDE, TOK), f32)
    for o in range(NCX):
        j = row - starts[:, o : o + 1]
        local = before[:, o : o + 1] + j
        here = jnp.where(local < HALF, local + o * HALF, local + ((2 * NCX - 1 - o) * HALF - HALF))
        pos = jnp.where((j >= 0) & (j < sizes[:, o : o + 1]), here, pos)
    loader, lane = iota((SIDE, TOK), 0), iota((SIDE, TOK), 1)
    rest = jnp.zeros((SIDE, TOK), f32)
    for r in range(REST):
        here = (loader == lane // REST) & (lane % REST == r)
        rest = jnp.where(here, pos[:, MAIN + r : MAIN + r + 1], rest)
    pos_ref[:SIDE, :] = jnp.where(lane < MAIN, pos, FAR)
    rest = jnp.where(lane[:1] < SIDE * REST, jnp.sum(rest, axis=0, keepdims=True), FAR)
    pos_ref[SIDE:, :] = jnp.broadcast_to(rest, (8, TOK))
    for i in range(SIDE):
        all_ref[(i + 1) * TOK - 16 : (i + 1) * TOK, :] = jnp.zeros((16, 2 * HD), bf16)
        all_ref[i * TOK : i * TOK + MAIN, :] = kv_ref[i]
    all_ref[SIDE * TOK : SIDE * TOK + SIDE * REST, :] = rest_ref[...]
    all_ref[SIDE * TOK + SIDE * REST :, :] = jnp.zeros((TOK - SIDE * REST, 2 * HD), bf16)


def unpack_kernel(counts_ref, got_ref, out_ref, rest_ref):
    me = lax.axis_index("ctx")
    n = NCX * PARTS
    got = got_ref[...].reshape(n, SPAN)
    counts = counts_ref[...].astype(f32)
    mine = jnp.sum(jnp.where(iota((NCX, NCX), 1) == me, counts, 0.0), axis=1, keepdims=True)
    src_of, src = iota((NCX, n), 1) // PARTS, iota((NCX, n), 0)
    before = jnp.sum(jnp.where(src < src_of, mine, 0.0), axis=0, keepdims=True)
    count = jnp.sum(jnp.where(src == src_of, mine, 0.0), axis=0, keepdims=True)
    part = iota((1, n), 1) % PARTS
    row = iota((TOK, n), 0).astype(f32)
    wide = GROUP * HD
    query = jnp.zeros((TOK, wide), f32)
    for c in range(SLOT // PARTS):
        j = (part * (SLOT // PARTS) + c).astype(f32)
        pick = jnp.where(row == jnp.where(j < count, before + j, -1.0), 1.0, 0.0).astype(bf16)
        query = query + jnp.dot(pick, got[:, c * wide : (c + 1) * wide], preferred_element_type=f32)
    for h in range(GROUP):
        out_ref[h * TOK : (h + 1) * TOK, :] = query[:, h * HD : (h + 1) * HD].astype(bf16)
    loader, slot = iota((SIDE, n), 0), iota((SIDE, n), 1)
    for c in range(PARTS):
        pick = jnp.where(slot == (2 * loader + me % 2) * PARTS + c, 1.0, 0.0).astype(bf16)
        rest = jnp.dot(pick, got[:, SPAN - HD :], preferred_element_type=f32)
        rest_ref[:, c * HD : (c + 1) * HD] = rest.astype(bf16)


def attend_kernel(flip, docs_ref, pos_ref, q_ref, kv_ref, out_ref, s_ref, p_ref, bias_ref):
    me = lax.axis_index("ctx")
    owner = me + flip * (1 - 2 * (me % 2))
    q_id = iota((TOK, HD), 0)
    q_pos = jnp.where(q_id < HALF, owner * HALF + q_id, (2 * NCX - 1 - owner) * HALF + q_id - HALF)
    q_first = jnp.zeros((TOK, HD), i32)
    end = jnp.int32(0)
    for d in range(docs_ref.shape[0]):
        end = end + docs_ref[d]
        q_first = jnp.where(q_pos >= end, end, q_first)
    q_pos, q_first = q_pos.astype(f32), q_first.astype(f32)

    tops = [jnp.full((TOK, HD), NEG, f32) for _ in range(GROUP)]
    for i in range(0, SIDE + 1, 2):
        n = min(2, SIDE + 1 - i)
        for c in range(n):
            k_pos = pos_ref[i + c : i + c + 1, :]
            bias_ref[:, c * TOK : (c + 1) * TOK] = jnp.where((k_pos <= q_pos) & (k_pos >= q_first), 0.0, NEG)
        s = lax.dot_general(
            q_ref[...],
            kv_ref[i * TOK : (i + n) * TOK, :HD],
            (((1,), (1,)), ((), ())),
            preferred_element_type=f32,
        )
        for h in range(GROUP):
            for c in range(n):
                cols = slice(c * TOK, (c + 1) * TOK)
                part = s[h * TOK : (h + 1) * TOK, cols] + bias_ref[:, cols]
                s_ref[h * TOK : (h + 1) * TOK, (i + c) * TOK : (i + c + 1) * TOK] = part
                tops[h] = jnp.maximum(tops[h], part)
    lane = iota((TOK, HD), 1)
    stats = jnp.zeros((TOK, HD), f32)
    totals = []
    for h in range(GROUP):
        top = jnp.broadcast_to(jnp.max(tops[h], axis=1, keepdims=True), (TOK, HD))
        total = jnp.zeros((TOK, HD), f32)
        for i in range(SIDE + 1):
            cols = slice(i * TOK, (i + 1) * TOK)
            e = jnp.exp2((s_ref[h * TOK : (h + 1) * TOK, cols] - top) * C2)
            total = total + e
            p_ref[h * TOK : (h + 1) * TOK, cols] = e.astype(bf16)
        total = jnp.broadcast_to(jnp.sum(total, axis=1, keepdims=True), (TOK, HD))
        totals.append(total)
        for k, value in ((h, top), (GROUP + h, total)):
            if flip:
                for term in range(3):
                    piece = value.astype(bf16).astype(f32)
                    stats = jnp.where(lane == term * 2 * GROUP + k, piece, stats)
                    value = value - piece
            else:
                stats = jnp.where(lane == k, value, stats)
    acc = jnp.dot(p_ref[...], kv_ref[:, HD:], preferred_element_type=f32)
    for h in range(GROUP):
        rows = slice(h * TOK, (h + 1) * TOK)
        out_ref[rows, :] = (acc[rows] / totals[h]).astype(bf16) if flip else acc[rows]
    out_ref[GROUP * TOK :, :] = stats.astype(out_ref.dtype)


def join_kernel(a_ref, b_ref, out_ref):
    sa = a_ref[GROUP * TOK :, :]
    sb = b_ref[GROUP * TOK :, :].astype(f32)

    def stat(k):
        return sum(sb[:, term * 2 * GROUP + k : term * 2 * GROUP + k + 1] for term in range(3))

    for h in range(GROUP):
        top_a, top_b = sa[:, h : h + 1], stat(h)
        top = jnp.maximum(top_a, top_b)
        wa = jnp.exp2((top_a - top) * C2)
        wb = jnp.exp2((top_b - top) * C2) * stat(GROUP + h)
        total = sa[:, GROUP + h : GROUP + h + 1] * wa + wb
        wa, wb = wa / total, wb / total
        rows = slice(h * TOK, (h + 1) * TOK)
        out_ref[:, h * HD : (h + 1) * HD] = (a_ref[rows, :] * wa + b_ref[rows, :].astype(f32) * wb).astype(bf16)


VMEM = pl.BlockSpec(memory_space=pltpu.VMEM)
LIMIT = pltpu.CompilerParams(vmem_limit_bytes=24 * 2**20)
SMEM = pl.BlockSpec(memory_space=pltpu.SMEM)


def near(x):
    return pltpu.with_memory_space_constraint(x, pltpu.VMEM)


def swap(x):
    return lax.ppermute(x, "ctx", [(i, i ^ 1) for i in range(NCX)])


def attend(flip, doc_lengths, pos, query, key_value):
    span = KEYS + TOK
    return pl.pallas_call(
        functools.partial(attend_kernel, flip),
        out_shape=pltpu.VMEM((GROUP * TOK + TOK, HD), bf16 if flip else f32),
        in_specs=[SMEM, VMEM, VMEM, VMEM],
        out_specs=VMEM,
        scratch_shapes=[
            pltpu.VMEM((GROUP * TOK, span), f32),
            pltpu.VMEM((GROUP * TOK, span), bf16),
            pltpu.VMEM((TOK, 2 * TOK), f32),
        ],
        cost_estimate=pl.CostEstimate(
            flops=4 * GROUP * TOK * KEYS * HD, bytes_accessed=2 * KEYS * HD * 2, transcendentals=GROUP * TOK * KEYS
        ),
        compiler_params=LIMIT,
        name="attend_partner" if flip else "attend_own",
    )(doc_lengths, pos, query, key_value)


def body(queries, keys, values, counts, doc_lengths):
    wide = GROUP * HD
    packed, key_value = pl.pallas_call(
        pack_kernel,
        out_shape=(
            pltpu.VMEM((NCX, PARTS, SPAN), bf16),
            pltpu.VMEM((MAIN, 2 * HD), bf16),
        ),
        in_specs=[VMEM, VMEM, VMEM, VMEM],
        out_specs=(VMEM, VMEM),
        name="pack",
    )(counts, queries, keys, values)
    got = lax.all_to_all(
        packed, "ctx", split_axis=0, concat_axis=0, tiled=True
    )
    key_value = lax.all_gather(key_value, "ctx", axis=0, axis_index_groups=SIDES)
    got, key_value = lax.optimization_barrier((got, key_value))
    query, rest = pl.pallas_call(
        unpack_kernel,
        out_shape=(
            pltpu.VMEM((GROUP * TOK, HD), bf16),
            pltpu.VMEM((SIDE * REST, 2 * HD), bf16),
        ),
        in_specs=[VMEM, VMEM],
        out_specs=(VMEM, VMEM),
        compiler_params=LIMIT,
        name="unpack",
    )(counts, near(got))
    pos, key_value = pl.pallas_call(
        place_kernel,
        out_shape=(
            pltpu.VMEM((SIDE + 8, TOK), f32),
            pltpu.VMEM((KEYS + TOK, 2 * HD), bf16),
        ),
        in_specs=[VMEM, VMEM, VMEM],
        out_specs=(VMEM, VMEM),
        compiler_params=LIMIT,
        name="place",
    )(counts, near(key_value), near(rest))
    pos, query, key_value = near(pos), near(query), near(key_value)
    partner = attend(1, doc_lengths, pos, near(swap(query)), key_value)
    other = swap(partner)
    own = attend(0, doc_lengths, pos, query, key_value)
    return pl.pallas_call(
        join_kernel,
        out_shape=jax.ShapeDtypeStruct((TOK, wide), bf16),
        in_specs=[VMEM, VMEM],
        out_specs=VMEM,
        compiler_params=LIMIT,
        name="join",
    )(near(own), near(other))


def solution(mesh):
    placed = (
        P(("dp", "ctx"), "tp"),
        P(("dp", "ctx"), "tp"),
        P(("dp", "ctx"), "tp"),
        P("dp", None),
        P("dp"),
    )
    return jax.shard_map(
        body, mesh=mesh, in_specs=placed, out_specs=P(("dp", "ctx"), "tp"), check_vma=False
    )
```

```python
import functools

import jax
import jax.numpy as jnp
from jax import lax
from jax.experimental import pallas as pl
from jax.experimental.pallas import tpu as pltpu
from jax.sharding import PartitionSpec as P

HQ = 32
KVH = 8
HD = 128
GROUP = HQ // KVH
TOK = 128
HALF = 64
NCX = 32
SLOT = 8
SIDE = NCX // 2
KEYS = SIDE * TOK
MAIN = 127
REST = TOK - MAIN
PARTS = 2
SPAN = SLOT // PARTS * GROUP * HD + HD
C2 = 1.4426950408889634 / HD**0.5
NEG = -1e30
STEP = 4
FAR = 1e9
SIDES = [list(range(0, NCX, 2)), list(range(1, NCX, 2))]

f32 = jnp.float32
bf16 = jnp.bfloat16
i32 = jnp.int32


def iota(shape, dim):
    return lax.broadcasted_iota(i32, shape, dim)


def pack_kernel(counts_ref, q_ref, k_ref, v_ref, out_ref, kv_ref):
    me = lax.axis_index("ctx")
    row = counts_ref[pl.ds(me, 1), :].astype(f32)
    n = NCX * PARTS
    owner_of, owner = iota((n, NCX), 0) // PARTS, iota((n, NCX), 1)
    start = jnp.sum(jnp.where(owner < owner_of, row, 0.0), axis=1, keepdims=True)
    count = jnp.sum(jnp.where(owner == owner_of, row, 0.0), axis=1, keepdims=True)
    part = iota((n, 1), 0) % PARTS
    lane = iota((n, TOK), 1).astype(f32)
    pieces = []
    for c in range(SLOT // PARTS):
        j = (part * (SLOT // PARTS) + c).astype(f32)
        pick = jnp.where(lane == jnp.where(j < count, start + j, -1.0), 1.0, 0.0).astype(bf16)
        pieces.append(jnp.dot(pick, q_ref[...], preferred_element_type=f32).astype(bf16))
    last = jnp.where(part == 0, k_ref[MAIN:, :].astype(f32), v_ref[MAIN:, :].astype(f32))
    pieces.append(last.astype(bf16))
    out_ref[...] = jnp.concatenate(pieces, axis=1).reshape(NCX, PARTS, SPAN)
    kv_ref[:, :HD] = k_ref[:MAIN, :]
    kv_ref[:, HD:] = v_ref[:MAIN, :]


def place_kernel(docs_ref, counts_ref, kv_ref, rest_ref, bias_ref, all_ref):
    me = lax.axis_index("ctx")
    parity = me % 2
    counts = counts_ref[...].astype(f32)
    a, b = iota((NCX, NCX), 0), iota((NCX, NCX), 1)
    side = (iota((SIDE, NCX), 1) == 2 * iota((SIDE, NCX), 0) + parity).astype(f32)
    sizes = jnp.dot(side, counts, preferred_element_type=f32)
    starts = jnp.dot(sizes, (a < b).astype(f32), preferred_element_type=f32)
    upto = (b[:SIDE] < 2 * a[:SIDE] + parity).astype(f32)
    before = jnp.dot(upto, counts, preferred_element_type=f32)
    row = iota((SIDE, TOK), 1).astype(f32)
    pos = jnp.zeros((SIDE, TOK), f32)
    for o in range(NCX):
        j = row - starts[:, o : o + 1]
        local = before[:, o : o + 1] + j
        here = jnp.where(local < HALF, local + o * HALF, local + ((2 * NCX - 1 - o) * HALF - HALF))
        pos = jnp.where((j >= 0) & (j < sizes[:, o : o + 1]), here, pos)
    loader, lane = iota((SIDE, TOK), 0), iota((SIDE, TOK), 1)
    rest = jnp.zeros((SIDE, TOK), f32)
    for r in range(REST):
        here = (loader == lane // REST) & (lane % REST == r)
        rest = jnp.where(here, pos[:, MAIN + r : MAIN + r + 1], rest)
    pos = jnp.where(lane < MAIN, pos, FAR)
    rest = jnp.where(lane[:1] < SIDE * REST, jnp.sum(rest, axis=0, keepdims=True), FAR)
    for flip in range(2):
        owner = me + flip * (1 - 2 * parity)
        q_id = iota((TOK, HD), 0)
        q_pos = jnp.where(q_id < HALF, owner * HALF + q_id, (2 * NCX - 1 - owner) * HALF + q_id - HALF)
        q_first = jnp.zeros((TOK, HD), i32)
        end = jnp.int32(0)
        for d in range(docs_ref.shape[0]):
            end = end + docs_ref[d]
            q_first = jnp.where(q_pos >= end, end, q_first)
        q_pos, q_first = q_pos.astype(f32), q_first.astype(f32)
        for i in range(SIDE + 1):
            k_pos = pos[i : i + 1, :] if i < SIDE else rest
            seen = jnp.where((k_pos <= q_pos) & (k_pos >= q_first), 0.0, NEG)
            bias_ref[flip, i // 2, :, i % 2 * TOK : (i % 2 + 1) * TOK] = seen
    for i in range(SIDE):
        all_ref[(i + 1) * TOK - 16 : (i + 1) * TOK, :] = jnp.zeros((16, 2 * HD), bf16)
        all_ref[i * TOK : i * TOK + MAIN, :] = kv_ref[i]
    all_ref[SIDE * TOK : SIDE * TOK + SIDE * REST, :] = rest_ref[...]
    all_ref[SIDE * TOK + SIDE * REST :, :] = jnp.zeros((TOK - SIDE * REST, 2 * HD), bf16)


def unpack_kernel(counts_ref, got_ref, out_ref, rest_ref):
    me = lax.axis_index("ctx")
    n = NCX * PARTS
    got = got_ref[...].reshape(n, SPAN)
    counts = counts_ref[...].astype(f32)
    mine = jnp.sum(jnp.where(iota((NCX, NCX), 1) == me, counts, 0.0), axis=1, keepdims=True)
    src_of, src = iota((NCX, n), 1) // PARTS, iota((NCX, n), 0)
    before = jnp.sum(jnp.where(src < src_of, mine, 0.0), axis=0, keepdims=True)
    count = jnp.sum(jnp.where(src == src_of, mine, 0.0), axis=0, keepdims=True)
    part = iota((1, n), 1) % PARTS
    row = iota((TOK, n), 0).astype(f32)
    wide = GROUP * HD
    query = jnp.zeros((TOK, wide), f32)
    for c in range(SLOT // PARTS):
        j = (part * (SLOT // PARTS) + c).astype(f32)
        pick = jnp.where(row == jnp.where(j < count, before + j, -1.0), 1.0, 0.0).astype(bf16)
        query = query + jnp.dot(pick, got[:, c * wide : (c + 1) * wide], preferred_element_type=f32)
    for h in range(GROUP):
        out_ref[h * TOK : (h + 1) * TOK, :] = query[:, h * HD : (h + 1) * HD].astype(bf16)
    loader, slot = iota((SIDE, n), 0), iota((SIDE, n), 1)
    for c in range(PARTS):
        pick = jnp.where(slot == (2 * loader + me % 2) * PARTS + c, 1.0, 0.0).astype(bf16)
        rest = jnp.dot(pick, got[:, SPAN - HD :], preferred_element_type=f32)
        rest_ref[:, c * HD : (c + 1) * HD] = rest.astype(bf16)


def attend_kernel(flip, bias_ref, q_ref, kv_ref, out_ref, s_ref, top_ref, sum_ref, acc_ref):
    two = 2 * TOK

    def scores(pair, i, n):
        s = lax.dot_general(
            q_ref[pair * two : (pair + 1) * two, :],
            kv_ref[pl.ds(i * two, n), :HD],
            (((1,), (1,)), ((), ())),
            preferred_element_type=f32,
        )
        for h in range(2):
            top = top_ref[2 * pair + h]
            for c in range(0, n, TOK):
                part = s[h * TOK : (h + 1) * TOK, c : c + TOK] + bias_ref[flip, i, :, c : c + TOK]
                s_ref[pair, i, h * TOK : (h + 1) * TOK, c : c + TOK] = part
                top = jnp.maximum(top, part)
            top_ref[2 * pair + h] = top

    def weights(pair, i, n):
        rows = []
        for h in range(2):
            top = top_ref[2 * pair + h]
            total = sum_ref[2 * pair + h]
            cols = []
            for c in range(0, n, TOK):
                e = jnp.exp2((s_ref[pair, i, h * TOK : (h + 1) * TOK, c : c + TOK] - top) * C2)
                total = total + e
                cols.append(e.astype(bf16))
            sum_ref[2 * pair + h] = total
            rows.append(jnp.concatenate(cols, axis=1))
        weight = jnp.concatenate(rows, axis=0)
        acc_ref[pair] += jnp.dot(weight, kv_ref[pl.ds(i * two, n), HD:], preferred_element_type=f32)

    def sweep(*steps):
        def trip(t, carry):
            for k in range(STEP):
                for step, pair in steps:
                    step(pair, t * STEP + k, two)
            return carry

        lax.fori_loop(0, SIDE // 2 // STEP, trip, 0)
        for step, pair in steps:
            step(pair, SIDE // 2, TOK)

    def settle(pair):
        for h in range(2 * pair, 2 * pair + 2):
            top_ref[h] = jnp.broadcast_to(jnp.max(top_ref[h], axis=1, keepdims=True), (TOK, HD))

    top_ref[...] = jnp.full(top_ref.shape, NEG, f32)
    sum_ref[...] = jnp.zeros(sum_ref.shape, f32)
    acc_ref[...] = jnp.zeros(acc_ref.shape, f32)
    sweep((scores, 0))
    settle(0)
    sweep((scores, 1), (weights, 0))
    settle(1)
    sweep((weights, 1))
    lane = iota((TOK, HD), 1)
    stats = jnp.zeros((TOK, HD), f32)
    for h in range(GROUP):
        total = jnp.broadcast_to(jnp.sum(sum_ref[h], axis=1, keepdims=True), (TOK, HD))
        stats = jnp.where(lane == h, top_ref[h], stats)
        stats = jnp.where(lane == GROUP + h, total, stats)
        acc = acc_ref[h // 2, h % 2 * TOK : (h % 2 + 1) * TOK, :]
        out_ref[h * TOK : (h + 1) * TOK, :] = (acc / total).astype(bf16) if flip else acc
    if flip:
        terms = jnp.zeros((TOK, HD), f32)
        for term in range(3):
            piece = stats.astype(bf16).astype(f32)
            terms = terms + (pltpu.roll(piece, term * 2 * GROUP, axis=1) if term else piece)
            stats = stats - piece
        stats = terms
    out_ref[GROUP * TOK :, :] = stats.astype(out_ref.dtype)


def join_kernel(a_ref, b_ref, out_ref):
    sa = a_ref[GROUP * TOK :, :]
    sb = b_ref[GROUP * TOK :, :].astype(f32)

    def stat(k):
        return sum(sb[:, term * 2 * GROUP + k : term * 2 * GROUP + k + 1] for term in range(3))

    for h in range(GROUP):
        top_a, top_b = sa[:, h : h + 1], stat(h)
        top = jnp.maximum(top_a, top_b)
        wa = jnp.exp2((top_a - top) * C2)
        wb = jnp.exp2((top_b - top) * C2) * stat(GROUP + h)
        total = sa[:, GROUP + h : GROUP + h + 1] * wa + wb
        wa, wb = wa / total, wb / total
        rows = slice(h * TOK, (h + 1) * TOK)
        out_ref[:, h * HD : (h + 1) * HD] = (a_ref[rows, :] * wa + b_ref[rows, :].astype(f32) * wb).astype(bf16)


VMEM = pl.BlockSpec(memory_space=pltpu.VMEM)
LIMIT = pltpu.CompilerParams(vmem_limit_bytes=24 * 2**20)
SMEM = pl.BlockSpec(memory_space=pltpu.SMEM)


def near(x):
    return pltpu.with_memory_space_constraint(x, pltpu.VMEM)


def swap(x):
    return lax.ppermute(x, "ctx", [(i, i ^ 1) for i in range(NCX)])


def attend(flip, bias, query, key_value):
    return pl.pallas_call(
        functools.partial(attend_kernel, flip),
        out_shape=pltpu.VMEM((GROUP * TOK + TOK, HD), bf16 if flip else f32),
        in_specs=[VMEM, VMEM, VMEM],
        out_specs=VMEM,
        scratch_shapes=[
            pltpu.VMEM((2, SIDE // 2 + 1, 2 * TOK, 2 * TOK), f32),
            pltpu.VMEM((GROUP, TOK, HD), f32),
            pltpu.VMEM((GROUP, TOK, HD), f32),
            pltpu.VMEM((2, 2 * TOK, HD), f32),
        ],
        cost_estimate=pl.CostEstimate(
            flops=4 * GROUP * TOK * KEYS * HD, bytes_accessed=2 * KEYS * HD * 2, transcendentals=GROUP * TOK * KEYS
        ),
        compiler_params=LIMIT,
        name="attend_partner" if flip else "attend_own",
    )(bias, query, key_value)


def body(queries, keys, values, counts, doc_lengths):
    wide = GROUP * HD
    packed, key_value = pl.pallas_call(
        pack_kernel,
        out_shape=(
            pltpu.VMEM((NCX, PARTS, SPAN), bf16),
            pltpu.VMEM((MAIN, 2 * HD), bf16),
        ),
        in_specs=[VMEM, VMEM, VMEM, VMEM],
        out_specs=(VMEM, VMEM),
        name="pack",
    )(counts, queries, keys, values)
    got = lax.all_to_all(
        packed, "ctx", split_axis=0, concat_axis=0, tiled=True
    )
    key_value = lax.all_gather(key_value, "ctx", axis=0, axis_index_groups=SIDES)
    got, key_value = lax.optimization_barrier((got, key_value))
    query, rest = pl.pallas_call(
        unpack_kernel,
        out_shape=(
            pltpu.VMEM((GROUP * TOK, HD), bf16),
            pltpu.VMEM((SIDE * REST, 2 * HD), bf16),
        ),
        in_specs=[VMEM, VMEM],
        out_specs=(VMEM, VMEM),
        compiler_params=LIMIT,
        name="unpack",
    )(counts, near(got))
    bias, key_value = pl.pallas_call(
        place_kernel,
        out_shape=(
            pltpu.VMEM((2, SIDE // 2 + 1, TOK, 2 * TOK), f32),
            pltpu.VMEM((KEYS + TOK, 2 * HD), bf16),
        ),
        in_specs=[SMEM, VMEM, VMEM, VMEM],
        out_specs=(VMEM, VMEM),
        compiler_params=LIMIT,
        name="place",
    )(doc_lengths, counts, near(key_value), near(rest))
    bias, query, key_value = near(bias), near(query), near(key_value)
    partner = attend(1, bias, near(swap(query)), key_value)
    other = swap(partner)
    own = attend(0, bias, query, key_value)
    return pl.pallas_call(
        join_kernel,
        out_shape=jax.ShapeDtypeStruct((TOK, wide), bf16),
        in_specs=[VMEM, VMEM],
        out_specs=VMEM,
        compiler_params=LIMIT,
        name="join",
    )(near(own), near(other))


def solution(mesh):
    placed = (
        P(("dp", "ctx"), "tp"),
        P(("dp", "ctx"), "tp"),
        P(("dp", "ctx"), "tp"),
        P("dp", None),
        P("dp"),
    )
    return jax.shard_map(
        body, mesh=mesh, in_specs=placed, out_specs=P(("dp", "ctx"), "tp"), check_vma=False
    )
```

```python
import functools

import jax
import jax.numpy as jnp
from jax import lax
from jax.experimental import pallas as pl
from jax.experimental.pallas import tpu as pltpu
from jax.sharding import PartitionSpec as P

HQ = 32
KVH = 8
HD = 128
GROUP = HQ // KVH
TOK = 128
HALF = 64
NCX = 32
SLOT = 8
SIDE = NCX // 2
KEYS = SIDE * TOK
MAIN = 127
REST = TOK - MAIN
PARTS = 2
SPAN = SLOT // PARTS * GROUP * HD + HD
C2 = 1.4426950408889634 / HD**0.5
NEG = -1e30
STEP = 4
FAR = 1e9
SIDES = [list(range(0, NCX, 2)), list(range(1, NCX, 2))]

f32 = jnp.float32
bf16 = jnp.bfloat16
i32 = jnp.int32


def iota(shape, dim):
    return lax.broadcasted_iota(i32, shape, dim)


def pack_kernel(counts_ref, q_ref, k_ref, v_ref, out_ref, kv_ref, near_ref):
    me = lax.axis_index("ctx")
    row = counts_ref[pl.ds(me, 1), :].astype(f32)
    n = NCX * PARTS
    owner_of, owner = iota((n, NCX), 0) // PARTS, iota((n, NCX), 1)
    start = jnp.sum(jnp.where(owner < owner_of, row, 0.0), axis=1, keepdims=True)
    count = jnp.sum(jnp.where(owner == owner_of, row, 0.0), axis=1, keepdims=True)
    part = iota((n, 1), 0) % PARTS
    lane = iota((n, TOK), 1).astype(f32)
    pieces = []
    for c in range(SLOT // PARTS):
        j = (part * (SLOT // PARTS) + c).astype(f32)
        pick = jnp.where(lane == jnp.where(j < count, start + j, -1.0), 1.0, 0.0).astype(bf16)
        pieces.append(jnp.dot(pick, q_ref[...], preferred_element_type=f32).astype(bf16))
    last = jnp.where(part == 0, k_ref[MAIN:, :].astype(f32), v_ref[MAIN:, :].astype(f32))
    pieces.append(last.astype(bf16))
    out_ref[...] = jnp.concatenate(pieces, axis=1).reshape(NCX, PARTS, SPAN)
    kv_ref[:, :HD] = k_ref[:MAIN, :]
    kv_ref[:, HD:] = v_ref[:MAIN, :]
    near_ref[...] = counts_ref[...]


def place_kernel(docs_ref, counts_ref, kv_ref, rest_ref, bias_ref, all_ref):
    me = lax.axis_index("ctx")
    parity = me % 2
    counts = counts_ref[...].astype(f32)
    a, b = iota((NCX, NCX), 0), iota((NCX, NCX), 1)
    side = (iota((SIDE, NCX), 1) == 2 * iota((SIDE, NCX), 0) + parity).astype(f32)
    sizes = jnp.dot(side, counts, preferred_element_type=f32)
    starts = jnp.dot(sizes, (a < b).astype(f32), preferred_element_type=f32)
    upto = (b[:SIDE] < 2 * a[:SIDE] + parity).astype(f32)
    before = jnp.dot(upto, counts, preferred_element_type=f32)
    row = iota((SIDE, TOK), 1).astype(f32)
    pos = jnp.zeros((SIDE, TOK), f32)
    for o in range(NCX):
        j = row - starts[:, o : o + 1]
        local = before[:, o : o + 1] + j
        here = jnp.where(local < HALF, local + o * HALF, local + ((2 * NCX - 1 - o) * HALF - HALF))
        pos = jnp.where((j >= 0) & (j < sizes[:, o : o + 1]), here, pos)
    loader, lane = iota((SIDE, TOK), 0), iota((SIDE, TOK), 1)
    rest = jnp.zeros((SIDE, TOK), f32)
    for r in range(REST):
        here = (loader == lane // REST) & (lane % REST == r)
        rest = jnp.where(here, pos[:, MAIN + r : MAIN + r + 1], rest)
    pos = jnp.where(lane < MAIN, pos, FAR)
    rest = jnp.where(lane[:1] < SIDE * REST, jnp.sum(rest, axis=0, keepdims=True), FAR)
    for flip in range(2):
        owner = me + flip * (1 - 2 * parity)
        q_id = iota((TOK, HD), 0)
        q_pos = jnp.where(q_id < HALF, owner * HALF + q_id, (2 * NCX - 1 - owner) * HALF + q_id - HALF)
        q_first = jnp.zeros((TOK, HD), i32)
        end = jnp.int32(0)
        for d in range(docs_ref.shape[0]):
            end = end + docs_ref[d]
            q_first = jnp.where(q_pos >= end, end, q_first)
        q_pos, q_first = q_pos.astype(f32), q_first.astype(f32)
        for i in range(SIDE + 1):
            k_pos = pos[i : i + 1, :] if i < SIDE else rest
            seen = jnp.where((k_pos <= q_pos) & (k_pos >= q_first), 0.0, NEG)
            bias_ref[flip, i // 2, :, i % 2 * TOK : (i % 2 + 1) * TOK] = seen
    for i in range(SIDE):
        all_ref[(i + 1) * TOK - 16 : (i + 1) * TOK, :] = jnp.zeros((16, 2 * HD), bf16)
        all_ref[i * TOK : i * TOK + MAIN, :] = kv_ref[i]
    all_ref[SIDE * TOK : SIDE * TOK + SIDE * REST, :] = rest_ref[...]
    all_ref[SIDE * TOK + SIDE * REST :, :] = jnp.zeros((TOK - SIDE * REST, 2 * HD), bf16)


def unpack_kernel(counts_ref, got_ref, out_ref, rest_ref):
    me = lax.axis_index("ctx")
    n = NCX * PARTS
    got = got_ref[...].reshape(n, SPAN)
    counts = counts_ref[...].astype(f32)
    mine = jnp.sum(jnp.where(iota((NCX, NCX), 1) == me, counts, 0.0), axis=1, keepdims=True)
    src_of, src = iota((NCX, n), 1) // PARTS, iota((NCX, n), 0)
    before = jnp.sum(jnp.where(src < src_of, mine, 0.0), axis=0, keepdims=True)
    count = jnp.sum(jnp.where(src == src_of, mine, 0.0), axis=0, keepdims=True)
    part = iota((1, n), 1) % PARTS
    row = iota((TOK, n), 0).astype(f32)
    wide = GROUP * HD
    query = jnp.zeros((TOK, wide), f32)
    for c in range(SLOT // PARTS):
        j = (part * (SLOT // PARTS) + c).astype(f32)
        pick = jnp.where(row == jnp.where(j < count, before + j, -1.0), 1.0, 0.0).astype(bf16)
        query = query + jnp.dot(pick, got[:, c * wide : (c + 1) * wide], preferred_element_type=f32)
    for h in range(GROUP):
        out_ref[h * TOK : (h + 1) * TOK, :] = query[:, h * HD : (h + 1) * HD].astype(bf16)
    loader, slot = iota((SIDE, n), 0), iota((SIDE, n), 1)
    for c in range(PARTS):
        pick = jnp.where(slot == (2 * loader + me % 2) * PARTS + c, 1.0, 0.0).astype(bf16)
        rest = jnp.dot(pick, got[:, SPAN - HD :], preferred_element_type=f32)
        rest_ref[:, c * HD : (c + 1) * HD] = rest.astype(bf16)


def attend_kernel(flip, bias_ref, q_ref, kv_ref, out_ref, s_ref, top_ref, sum_ref, acc_ref):
    two = 2 * TOK

    def scores(pair, i, n):
        s = lax.dot_general(
            q_ref[pair * two : (pair + 1) * two, :],
            kv_ref[pl.ds(i * two, n), :HD],
            (((1,), (1,)), ((), ())),
            preferred_element_type=f32,
        )
        for h in range(2):
            top = top_ref[2 * pair + h]
            for c in range(0, n, TOK):
                part = s[h * TOK : (h + 1) * TOK, c : c + TOK] + bias_ref[flip, i, :, c : c + TOK]
                s_ref[pair, i, h * TOK : (h + 1) * TOK, c : c + TOK] = part
                top = jnp.maximum(top, part)
            top_ref[2 * pair + h] = top

    def weights(pair, i, n):
        rows = []
        for h in range(2):
            top = top_ref[2 * pair + h]
            total = sum_ref[2 * pair + h]
            cols = []
            for c in range(0, n, TOK):
                e = jnp.exp2((s_ref[pair, i, h * TOK : (h + 1) * TOK, c : c + TOK] - top) * C2)
                total = total + e
                cols.append(e.astype(bf16))
            sum_ref[2 * pair + h] = total
            rows.append(jnp.concatenate(cols, axis=1))
        weight = jnp.concatenate(rows, axis=0)
        acc_ref[pair] += jnp.dot(weight, kv_ref[pl.ds(i * two, n), HD:], preferred_element_type=f32)

    def sweep(*steps):
        def trip(t, carry):
            for k in range(STEP):
                for step, pair in steps:
                    step(pair, t * STEP + k, two)
            return carry

        lax.fori_loop(0, SIDE // 2 // STEP, trip, 0)
        for step, pair in steps:
            step(pair, SIDE // 2, TOK)

    def settle(pair):
        for h in range(2 * pair, 2 * pair + 2):
            top_ref[h] = jnp.broadcast_to(jnp.max(top_ref[h], axis=1, keepdims=True), (TOK, HD))

    top_ref[...] = jnp.full(top_ref.shape, NEG, f32)
    sum_ref[...] = jnp.zeros(sum_ref.shape, f32)
    acc_ref[...] = jnp.zeros(acc_ref.shape, f32)
    sweep((scores, 0))
    settle(0)
    sweep((scores, 1), (weights, 0))
    settle(1)
    sweep((weights, 1))
    lane = iota((TOK, HD), 1)
    stats = jnp.zeros((TOK, HD), f32)
    for h in range(GROUP):
        total = jnp.broadcast_to(jnp.sum(sum_ref[h], axis=1, keepdims=True), (TOK, HD))
        stats = jnp.where(lane == h, top_ref[h], stats)
        stats = jnp.where(lane == GROUP + h, total, stats)
        acc = acc_ref[h // 2, h % 2 * TOK : (h % 2 + 1) * TOK, :]
        out_ref[h * TOK : (h + 1) * TOK, :] = (acc / total).astype(bf16) if flip else acc
    if flip:
        terms = jnp.zeros((TOK, HD), f32)
        for term in range(3):
            piece = stats.astype(bf16).astype(f32)
            terms = terms + (pltpu.roll(piece, term * 2 * GROUP, axis=1) if term else piece)
            stats = stats - piece
        stats = terms
    out_ref[GROUP * TOK :, :] = stats.astype(out_ref.dtype)


def join_kernel(a_ref, b_ref, out_ref):
    sa = a_ref[GROUP * TOK :, :]
    sb = b_ref[GROUP * TOK :, :].astype(f32)
    sb = sb + pltpu.roll(sb, HD - 2 * GROUP, axis=1) + pltpu.roll(sb, HD - 4 * GROUP, axis=1)
    top = jnp.maximum(sa, sb)
    wa, wb = jnp.exp2((sa - top) * C2), jnp.exp2((sb - top) * C2)
    wb = wb * pltpu.roll(sb, HD - GROUP, axis=1)
    total = wa * pltpu.roll(sa, HD - GROUP, axis=1) + wb
    wa, wb = wa / total, wb / total
    for h in range(GROUP):
        rows = slice(h * TOK, (h + 1) * TOK)
        half_a, half_b = a_ref[rows, :], b_ref[rows, :].astype(f32)
        out_ref[:, h * HD : (h + 1) * HD] = (half_a * wa[:, h : h + 1] + half_b * wb[:, h : h + 1]).astype(bf16)


VMEM = pl.BlockSpec(memory_space=pltpu.VMEM)
LIMIT = pltpu.CompilerParams(vmem_limit_bytes=24 * 2**20)
SMEM = pl.BlockSpec(memory_space=pltpu.SMEM)


def near(x):
    return pltpu.with_memory_space_constraint(x, pltpu.VMEM)


def swap(x):
    return lax.ppermute(x, "ctx", [(i, i ^ 1) for i in range(NCX)])


def attend(flip, bias, query, key_value):
    return pl.pallas_call(
        functools.partial(attend_kernel, flip),
        out_shape=pltpu.VMEM((GROUP * TOK + TOK, HD), bf16 if flip else f32),
        in_specs=[VMEM, VMEM, VMEM],
        out_specs=VMEM,
        scratch_shapes=[
            pltpu.VMEM((2, SIDE // 2 + 1, 2 * TOK, 2 * TOK), f32),
            pltpu.VMEM((GROUP, TOK, HD), f32),
            pltpu.VMEM((GROUP, TOK, HD), f32),
            pltpu.VMEM((2, 2 * TOK, HD), f32),
        ],
        cost_estimate=pl.CostEstimate(
            flops=4 * GROUP * TOK * KEYS * HD, bytes_accessed=2 * KEYS * HD * 2, transcendentals=GROUP * TOK * KEYS
        ),
        compiler_params=LIMIT,
        name="attend_partner" if flip else "attend_own",
    )(bias, query, key_value)


def body(queries, keys, values, counts, doc_lengths):
    wide = GROUP * HD
    packed, key_value, sizes = pl.pallas_call(
        pack_kernel,
        out_shape=(
            pltpu.VMEM((NCX, PARTS, SPAN), bf16),
            pltpu.VMEM((MAIN, 2 * HD), bf16),
            pltpu.VMEM((NCX, NCX), i32),
        ),
        in_specs=[VMEM, VMEM, VMEM, VMEM],
        out_specs=(VMEM, VMEM, VMEM),
        name="pack",
    )(counts, queries, keys, values)
    got = lax.all_to_all(
        packed, "ctx", split_axis=0, concat_axis=0, tiled=True
    )
    key_value = lax.all_gather(key_value, "ctx", axis=0, axis_index_groups=SIDES)
    got, key_value = lax.optimization_barrier((got, key_value))
    sizes = near(sizes)
    query, rest = pl.pallas_call(
        unpack_kernel,
        out_shape=(
            pltpu.VMEM((GROUP * TOK, HD), bf16),
            pltpu.VMEM((SIDE * REST, 2 * HD), bf16),
        ),
        in_specs=[VMEM, VMEM],
        out_specs=(VMEM, VMEM),
        compiler_params=LIMIT,
        name="unpack",
    )(sizes, near(got))
    bias, key_value = pl.pallas_call(
        place_kernel,
        out_shape=(
            pltpu.VMEM((2, SIDE // 2 + 1, TOK, 2 * TOK), f32),
            pltpu.VMEM((KEYS + TOK, 2 * HD), bf16),
        ),
        in_specs=[SMEM, VMEM, VMEM, VMEM],
        out_specs=(VMEM, VMEM),
        compiler_params=LIMIT,
        name="place",
    )(doc_lengths, sizes, near(key_value), near(rest))
    bias, query, key_value = near(bias), near(query), near(key_value)
    partner = attend(1, bias, near(swap(query)), key_value)
    other = swap(partner)
    own = attend(0, bias, query, key_value)
    return pl.pallas_call(
        join_kernel,
        out_shape=jax.ShapeDtypeStruct((TOK, wide), bf16),
        in_specs=[VMEM, VMEM],
        out_specs=VMEM,
        compiler_params=LIMIT,
        name="join",
    )(near(own), near(other))


def solution(mesh):
    placed = (
        P(("dp", "ctx"), "tp"),
        P(("dp", "ctx"), "tp"),
        P(("dp", "ctx"), "tp"),
        P("dp", None),
        P("dp"),
    )
    return jax.shard_map(
        body, mesh=mesh, in_specs=placed, out_specs=P(("dp", "ctx"), "tp"), check_vma=False
    )
```
